512 devices in a mesh: row: 16 (over y, x), adp: 32 (over z, core).
Axes of the slice: x: 4, y: 4, z: 16, core: 2. Of those that a mesh axis runs over, the one named last changes fastest.
Arguments:
- tokens: bfloat16 [8192, 8192], P('row', 'adp'), may hold values from -6 to 6
- query_base_weight: bfloat16 [8192, 8192], P(None, 'adp'), may hold values from -0.0625 to 0.0625
- adapter_down_weight: bfloat16 [32, 16, 8192], P('adp'), may hold values from -0.0625 to 0.0625
- adapter_up_weight: bfloat16 [32, 16, 8192], P('adp'), may hold values from -1.5 to 1.5
- row_adapter_index: int32 [8192, 1], P('row'), may hold values from 0 to 31; in each aligned block of 512 rows (0 to 511, 512 to 1023, ...) at most 64 rows name the same one
Outputs:
- queries: bfloat16 [8192, 8192], P('row', 'adp')
The draws below stay inside these ranges and needn't reach their ends.
Inputs may be any that keep to these rules, and one draw needn't show every extreme that they name: `row_adapter_index`: among the 512 rows of one index of row, no adapter is used by more than 64 rows, and some adapter is used by exactly 64 rows; every adapter is used by some row.
All inputs are finite; a program needn't handle non-finite values.
Results may differ from the reference program's by a relative error of at most 0.0055.
Values may be sent and summed in bfloat16 or wider, within the bound.
No kernel may reach another device: no remote copies, remote signals or barrier semaphores. Data moves between devices by JAX's collectives and lax.ppermute only.
A program may use at most 64 MiB of HBM per device.

```python
import math
import jax
import jax.numpy as jnp
import numpy as np
from jax import lax

MODEL_WIDTH = 8192
ADAPTER_RANK = 16
SCALE_NUMERATOR = 32
ROW_DEV = 512
ADAPTER_COUNT = 32
CAP = 64
ROWS = 8192


def shard_levels(key, dims, cuts, low, top_value):
    loudness, own = 1.0, jax.random.fold_in(key, 6)
    for axis_at, parts in cuts:
        heights = jnp.exp(jax.random.uniform(jax.random.fold_in(own, axis_at), (parts,), jnp.float32, low / len(cuts), top_value / len(cuts)))
        loudness = loudness * jnp.repeat(heights, dims[axis_at] // parts).reshape([-1 if axis == axis_at else 1 for axis in range(len(dims))])
    return loudness


def routed_block(stream_key, own, number, rows, number_of, top, limit, lean):
    sequence = jax.random.permutation(stream_key, number_of)
    packed, common = shares(number_of, rows * top, limit, lean, True), shares(number_of, rows * top, limit, lean, False)
    places = jnp.arange(number_of)

    def named(sizes, turn):
        used = int((sizes > 0).sum())
        fixed = max(1, used // 4)
        shifted = fixed + (places - fixed + turn * (used - fixed)) % max(1, number_of - fixed)
        return jnp.zeros((number_of,), jnp.int32).at[sequence[jnp.where(places < fixed, places, shifted)]].set(jnp.asarray(sizes, jnp.int32))

    sizes = jnp.where(number % 4 == 0, named(packed, number // 4), named(common, number - number // 4 - 1))
    mixed = jax.random.permutation(jax.random.fold_in(own, 3), number_of)
    source_of, receiver = mixed[0:number_of // 2 * 2:2], mixed[1:number_of // 2 * 2:2]
    room = jnp.minimum(sizes[source_of] - 1, limit - sizes[receiver]) // 2
    room = jnp.where((source_of == sequence[0]) | (receiver == sequence[0]) | (sizes[receiver] == 0), 0, jnp.maximum(room, 0))
    shifted = jax.random.randint(jax.random.fold_in(own, 4), (number_of // 2,), 0, 1 << 20) % (room + 1)
    sizes = sizes.at[source_of].add(-shifted).at[receiver].add(shifted)
    items = jnp.searchsorted(jnp.cumsum(sizes), jnp.arange(rows * top), side="right").astype(jnp.int32)
    grid = items.reshape(top, rows).T
    grid = grid[jax.random.permutation(jax.random.fold_in(own, 1), rows)]
    turn = jax.random.randint(jax.random.fold_in(own, 2), (rows, 1), 0, top)
    return jnp.take_along_axis(grid, (jnp.arange(top)[None, :] + turn) % top, axis=1)


def shares(number_of, total, bound, slope, full):
    portions = [(1 << 20) // math.isqrt(rank ** slope) + 1 for rank in range(1, number_of + 1)]
    largest = bound if full else min(bound, max(-(-total // number_of), total * portions[0] // sum(portions)))
    least = 1 if total - largest >= number_of - 1 else 0
    given, spare = [largest] + [least] * (number_of - 1), total - largest - least * (number_of - 1)
    while spare > 0:
        free = [i for i in range(1, number_of) if given[i] < largest] or [i for i in range(1, number_of) if given[i] < bound]
        mass, left = sum([portions[i] for i in free]), spare
        for i in free:
            extra = min(bound - given[i], max(1, left * portions[i] // mass), spare)
            given[i] = given[i] + extra
            spare = spare - extra
    return np.array(given)


def bell_draw(own_key, shape, deviation, bound, shards=(), kind=jnp.bfloat16):
    entries = deviation * jax.random.normal(own_key, shape, jnp.float32)
    if shards:
        entries = entries * shard_levels(own_key, shape, shards, -0.22, 0.18)
    return jnp.clip(entries, -bound, bound).astype(kind)


def setup_inputs(seed: int = 0) -> dict:
    key_of = jax.random.split(jax.random.key(seed), 6)
    tokens = bell_draw(key_of[0], (ROWS, MODEL_WIDTH), 1.0, 6.0, ((0, 16), (1, 32)))
    query_base_weight = bell_draw(key_of[1], (MODEL_WIDTH, MODEL_WIDTH), MODEL_WIDTH ** -0.5, 0.0625, ((1, 32),))
    adapter_down_weight = bell_draw(key_of[2], (ADAPTER_COUNT, ADAPTER_RANK, MODEL_WIDTH), MODEL_WIDTH ** -0.5, 0.0625, ((0, 32),))
    adapter_up_weight = bell_draw(key_of[3], (ADAPTER_COUNT, ADAPTER_RANK, MODEL_WIDTH), ADAPTER_RANK ** -0.5, 1.5, ((0, 32),))
    row_adapter_index_keys = jax.random.split(jax.random.fold_in(key_of[4], 1), ROWS // ROW_DEV)
    row_adapter_index_turns = jax.random.permutation(jax.random.fold_in(key_of[4], 3), ROWS // ROW_DEV)
    row_adapter_index = jax.vmap(lambda own, number: routed_block(jax.random.fold_in(key_of[4], 2), own, number, ROW_DEV, ADAPTER_COUNT, 1, CAP, 2))(row_adapter_index_keys, row_adapter_index_turns).reshape((ROWS, 1))
    return {"tokens": tokens, "query_base_weight": query_base_weight, "adapter_down_weight": adapter_down_weight, "adapter_up_weight": adapter_up_weight, "row_adapter_index": row_adapter_index}


def reference(tokens, query_base_weight, adapter_down_weight, adapter_up_weight, row_adapter_index):
    base_out = jnp.dot(tokens, query_base_weight, preferred_element_type=jnp.float32)
    down_weight_flat = adapter_down_weight.reshape(ADAPTER_COUNT * ADAPTER_RANK, MODEL_WIDTH)
    down_sums = lax.dot_general(tokens, down_weight_flat, (((1,), (1,)), ((), ())), preferred_element_type=jnp.float32)
    chosen = row_adapter_index[:, 0:1] == jnp.arange(ADAPTER_COUNT, dtype=jnp.int32)[None, :]
    expanded = jnp.repeat(chosen, ADAPTER_RANK, axis=1)
    rank_rows = jnp.where(expanded, down_sums, jnp.zeros_like(down_sums)).astype(jnp.bfloat16)
    up_weight_flat = adapter_up_weight.reshape(ADAPTER_COUNT * ADAPTER_RANK, MODEL_WIDTH)
    update = (jnp.dot(rank_rows, up_weight_flat, preferred_element_type=jnp.float32) * (SCALE_NUMERATOR / ADAPTER_RANK)).astype(jnp.bfloat16)
    update = lax.optimization_barrier(update)
    return (base_out + update.astype(jnp.float32)).astype(jnp.bfloat16)
```

```python
import jax
import jax.numpy as jnp
from jax import lax
from jax.experimental import pallas as pl
from jax.experimental.pallas import tpu as pltpu
from jax.sharding import PartitionSpec as P

ADAPTER_RANK = 16
SCALE_NUMERATOR = 32


def _sum_kernel(x_ref, w_ref, o_ref):
    part = jnp.dot(x_ref[0], w_ref[0], preferred_element_type=jnp.float32)

    @pl.when(pl.program_id(0) == 0)
    def _():
        o_ref[...] = part

    @pl.when(pl.program_id(0) > 0)
    def _():
        o_ref[...] += part


def _block_sum(x, w):
    steps, rows, width = x.shape
    cols = w.shape[2]
    return pl.pallas_call(
        _sum_kernel,
        grid=(steps,),
        in_specs=[
            pl.BlockSpec((1, rows, width), lambda i: (i, 0, 0)),
            pl.BlockSpec((1, width, cols), lambda i: (i, 0, 0)),
        ],
        out_specs=pl.BlockSpec((rows, cols), lambda i: (0, 0)),
        out_shape=jax.ShapeDtypeStruct((rows, cols), jnp.float32),
        cost_estimate=pl.CostEstimate(
            flops=2 * steps * rows * width * cols,
            bytes_accessed=2 * steps * width * (rows + cols) + 4 * rows * cols,
            transcendentals=0,
        ),
    )(x, w)


def shards(tokens, query_base_weight, adapter_down_weight, adapter_up_weight, row_adapter_index):
    rows, width = tokens.shape
    total_width, cols = query_base_weight.shape
    groups = lax.axis_size("adp")
    chips = groups // 2
    rank = adapter_down_weight.shape[1]
    adapters = groups
    core = lax.axis_index("adp") % 2
    row = lax.axis_index("row")
    scale = SCALE_NUMERATOR / ADAPTER_RANK
    same_core = [[2 * z + c for z in range(chips)] for c in range(2)]
    swap = [(a, a ^ 1) for a in range(groups)]

    gathered = lax.all_gather(tokens, "adp", axis=0, tiled=False, axis_index_groups=same_core)

    by_core = query_base_weight.reshape(chips, 2, width, cols)
    mine = lax.dynamic_slice_in_dim(by_core, core, 1, 1)[:, 0]
    theirs = lax.dynamic_slice_in_dim(by_core, 1 - core, 1, 1)[:, 0]
    partner = lax.ppermute(theirs, "adp", swap)

    tables = jnp.concatenate(
        [
            lax.dynamic_slice_in_dim(adapter_down_weight[0], row, 1, 0),
            lax.dynamic_slice_in_dim(adapter_up_weight[0], row, 1, 0),
        ],
        axis=0,
    )
    pieces = tables.reshape(2, groups, width).transpose(1, 0, 2)
    pieces = lax.all_to_all(pieces, "adp", split_axis=0, concat_axis=0, tiled=True)
    pieces = lax.all_gather(pieces, "row", axis=0, tiled=False)
    down = pieces[:, :, 0, :].reshape(rank * adapters, width)
    up = pieces[:, :, 1, :].reshape(rank * adapters, cols)

    chosen = (
        row_adapter_index[:, 0][None, :] == jnp.arange(adapters, dtype=jnp.int32)[:, None]
    )
    sums = lax.dot_general(
        down, tokens, (((1,), (1,)), ((), ())), preferred_element_type=jnp.float32
    ).reshape(rank, adapters, rows)
    sums = jnp.where(chosen[None], sums, 0.0).sum(axis=1)
    sums = sums + lax.ppermute(sums, "adp", swap)
    sums = lax.all_gather(sums, "adp", axis=0, tiled=False, axis_index_groups=same_core)
    ranks = sums.sum(axis=0).astype(jnp.bfloat16)
    spread = jnp.where(chosen[None], ranks[:, None, :], jnp.zeros((), jnp.bfloat16))
    update = (
        lax.dot_general(
            spread.reshape(rank * adapters, rows),
            up,
            (((0,), (0,)), ((), ())),
            preferred_element_type=jnp.float32,
        )
        * scale
    ).astype(jnp.bfloat16)

    other = _block_sum(gathered, partner)
    other = lax.ppermute(other, "adp", swap)
    own = _block_sum(gathered, mine)
    return (own + other + update.astype(jnp.float32)).astype(jnp.bfloat16)


def solution(mesh):
    return jax.shard_map(
        shards,
        mesh=mesh,
        in_specs=(
            P("row", "adp"),
            P(None, "adp"),
            P("adp", None, None),
            P("adp", None, None),
            P("row", None),
        ),
        out_specs=P("row", "adp"),
        check_vma=False,
    )
```

```python
import jax
import jax.numpy as jnp
from jax import lax
from jax.experimental import pallas as pl
from jax.experimental.pallas import tpu as pltpu
from jax.experimental.layout import Layout, with_layout_constraint
from jax.sharding import PartitionSpec as P

ADAPTER_RANK = 16
SCALE_NUMERATOR = 32


def _block_sum(x, w):
    return lax.dot_general(
        x, w, (((0, 2), (0, 1)), ((), ())), preferred_element_type=jnp.float32
    )


def shards(tokens, query_base_weight, adapter_down_weight, adapter_up_weight, row_adapter_index):
    rows, width = tokens.shape
    total_width, cols = query_base_weight.shape
    groups = lax.axis_size("adp")
    chips = groups // 2
    rank = adapter_down_weight.shape[1]
    adapters = groups
    core = lax.axis_index("adp") % 2
    row = lax.axis_index("row")
    scale = SCALE_NUMERATOR / ADAPTER_RANK
    same_core = [[2 * z + c for z in range(chips)] for c in range(2)]
    swap = [(a, a ^ 1) for a in range(groups)]

    gathered = lax.all_gather(tokens, "adp", axis=0, tiled=False, axis_index_groups=same_core)

    near = 4
    share = rank // near
    first = (row % near) * share
    pieces = jnp.stack(
        [
            lax.dynamic_slice_in_dim(adapter_down_weight[0], first, share, 0),
            lax.dynamic_slice_in_dim(adapter_up_weight[0], first, share, 0),
        ]
    )
    pieces = pieces.reshape(2 * share, groups, width).transpose(1, 0, 2)
    pieces, query_base_weight = lax.optimization_barrier((pieces, query_base_weight))
    pieces = lax.all_to_all(pieces, "adp", split_axis=0, concat_axis=0, tiled=True)
    pieces = pieces.reshape(adapters, 2, share, width).transpose(1, 2, 0, 3)
    lines = [[near * y + x for x in range(near)] for y in range(lax.axis_size("row") // near)]
    pieces = lax.all_gather(pieces, "row", axis=0, tiled=False, axis_index_groups=lines)
    down = pieces[:, 0].reshape(rank * adapters, width)
    up = pieces[:, 1].reshape(rank * adapters, cols)

    by_core = query_base_weight.reshape(chips, 2, width, cols)
    theirs = lax.dynamic_slice_in_dim(by_core, 1 - core, 1, 1)[:, 0]
    theirs = with_layout_constraint(theirs, Layout(major_to_minor=(0, 1, 2)))
    partner = lax.ppermute(theirs, "adp", swap)
    partner = with_layout_constraint(partner, Layout(major_to_minor=(0, 1, 2)))

    chosen = (
        row_adapter_index[:, 0][None, :] == jnp.arange(adapters, dtype=jnp.int32)[:, None]
    )
    sums = lax.dot_general(
        down, tokens, (((1,), (1,)), ((), ())), preferred_element_type=jnp.float32
    ).reshape(rank, adapters, rows)
    sums = jnp.where(chosen[None], sums, 0.0).sum(axis=1)
    sums = sums + lax.ppermute(sums, "adp", swap)
    sums = lax.all_gather(sums, "adp", axis=0, tiled=False, axis_index_groups=same_core)
    ranks = sums.sum(axis=0).astype(jnp.bfloat16)
    spread = jnp.where(chosen[None], ranks[:, None, :], jnp.zeros((), jnp.bfloat16))
    update = (
        lax.dot_general(
            spread.reshape(rank * adapters, rows),
            up,
            (((0,), (0,)), ((), ())),
            preferred_element_type=jnp.float32,
        )
        * scale
    ).astype(jnp.bfloat16)
    update = lax.optimization_barrier(update)

    other = _block_sum(gathered, partner)
    other = lax.ppermute(other, "adp", swap)
    own = _block_sum(gathered, lax.dynamic_slice_in_dim(by_core, core, 1, 1)[:, 0])
    return (own + other + update.astype(jnp.float32)).astype(jnp.bfloat16)


def solution(mesh):
    return jax.shard_map(
        shards,
        mesh=mesh,
        in_specs=(
            P("row", "adp"),
            P(None, "adp"),
            P("adp", None, None),
            P("adp", None, None),
            P("row", None),
        ),
        out_specs=P("row", "adp"),
        check_vma=False,
    )
```

```python
import jax
import jax.numpy as jnp
from jax import lax
from jax.experimental.layout import Layout, with_layout_constraint
from jax.sharding import PartitionSpec as P

ADAPTER_RANK = 16
SCALE_NUMERATOR = 32


def _block_sum(x, w):
    return lax.dot_general(
        w, x, (((0, 1), (0, 2)), ((), ())), preferred_element_type=jnp.float32
    )


def shards(tokens, query_base_weight, adapter_down_weight, adapter_up_weight, row_adapter_index):
    rows, width = tokens.shape
    _, cols = query_base_weight.shape
    groups = lax.axis_size("adp")
    chips = groups // 2
    rank = adapter_down_weight.shape[1]
    adapters = groups
    core = lax.axis_index("adp") % 2
    row = lax.axis_index("row")
    scale = SCALE_NUMERATOR / ADAPTER_RANK
    same_core = [[2 * z + c for z in range(chips)] for c in range(2)]
    swap = [(a, a ^ 1) for a in range(groups)]

    gathered = lax.all_gather(tokens, "adp", axis=0, tiled=False, axis_index_groups=same_core)

    near = 4
    share = rank // near
    first = (row % near) * share
    pieces = jnp.stack(
        [
            lax.dynamic_slice_in_dim(adapter_down_weight[0], first, share, 0),
            lax.dynamic_slice_in_dim(adapter_up_weight[0], first, share, 0),
        ]
    )
    pieces = pieces.reshape(2 * share, groups, width).transpose(1, 0, 2)
    pieces = lax.all_to_all(pieces, "adp", split_axis=0, concat_axis=0, tiled=True)
    pieces = pieces.reshape(adapters, 2, share, width).transpose(1, 2, 0, 3)
    lines = [[near * y + x for x in range(near)] for y in range(lax.axis_size("row") // near)]
    pieces = lax.all_gather(pieces, "row", axis=0, tiled=False, axis_index_groups=lines)
    down = pieces[:, 0].reshape(rank * adapters, width)
    up = pieces[:, 1].reshape(rank * adapters, cols)

    by_core = query_base_weight.reshape(chips, 2, width, cols)
    theirs = lax.dynamic_slice_in_dim(by_core, 1 - core, 1, 1)[:, 0]
    mine = lax.dynamic_slice_in_dim(by_core, core, 1, 1)[:, 0]
    mine, theirs = lax.optimization_barrier((mine, theirs))
    theirs = with_layout_constraint(theirs, Layout(major_to_minor=(0, 1, 2)))
    partner = lax.ppermute(theirs, "adp", swap)
    partner = with_layout_constraint(partner, Layout(major_to_minor=(0, 1, 2)))

    chosen = (
        row_adapter_index[:, 0][None, :] == jnp.arange(adapters, dtype=jnp.int32)[:, None]
    )
    sums = lax.dot_general(
        down, tokens, (((1,), (1,)), ((), ())), preferred_element_type=jnp.float32
    ).reshape(rank, adapters, rows)
    sums = jnp.where(chosen[None], sums, 0.0).sum(axis=1)
    sums = sums + lax.ppermute(sums, "adp", swap)
    sums = lax.all_gather(sums, "adp", axis=0, tiled=False, axis_index_groups=same_core)
    ranks = sums.sum(axis=0).astype(jnp.bfloat16)
    spread = jnp.where(chosen[None], ranks[:, None, :], jnp.zeros((), jnp.bfloat16))
    update = (
        lax.dot_general(
            up,
            spread.reshape(rank * adapters, rows),
            (((0,), (0,)), ((), ())),
            preferred_element_type=jnp.float32,
        )
        * scale
    ).astype(jnp.bfloat16)
    update = lax.optimization_barrier(update)

    other = _block_sum(gathered, partner)
    other = lax.ppermute(other, "adp", swap)
    own = _block_sum(gathered, mine)
    return (own + other + update.astype(jnp.float32)).astype(jnp.bfloat16).T


def solution(mesh):
    return jax.shard_map(
        shards,
        mesh=mesh,
        in_specs=(
            P("row", "adp"),
            P(None, "adp"),
            P("adp", None, None),
            P("adp", None, None),
            P("row", None),
        ),
        out_specs=P("row", "adp"),
        check_vma=False,
    )
```

```python
import jax
import jax.numpy as jnp
from jax import lax
from jax.experimental.layout import Layout, with_layout_constraint
from jax.sharding import PartitionSpec as P

ADAPTER_RANK = 16
SCALE_NUMERATOR = 32


def _block_sum(x, w):
    y = lax.dot_general(
        x, w, (((0, 2), (0, 1)), ((), ())), preferred_element_type=jnp.float32
    )
    return with_layout_constraint(y, Layout(major_to_minor=(0, 1)))


def shards(tokens, query_base_weight, adapter_down_weight, adapter_up_weight, row_adapter_index):
    rows, width = tokens.shape
    _, cols = query_base_weight.shape
    groups = lax.axis_size("adp")
    chips = groups // 2
    rank = adapter_down_weight.shape[1]
    adapters = groups
    core = (lax.axis_index("adp") + lax.axis_index("adp") // 2) % 2
    row = lax.axis_index("row")
    scale = SCALE_NUMERATOR / ADAPTER_RANK
    same_core = [[2 * z + (z + c) % 2 for z in range(chips)] for c in range(2)]
    swap = [(a, a ^ 1) for a in range(groups)]

    gathered = lax.all_gather(tokens, "adp", axis=0, tiled=False, axis_index_groups=same_core)

    near = 4
    share = rank // near
    first = (row % near) * share
    pieces = jnp.stack(
        [
            lax.dynamic_slice_in_dim(adapter_down_weight[0], first, share, 0),
            lax.dynamic_slice_in_dim(adapter_up_weight[0], first, share, 0),
        ]
    )
    pieces = pieces.reshape(2 * share, groups, width).transpose(1, 0, 2)
    pieces = lax.all_to_all(pieces, "adp", split_axis=0, concat_axis=0, tiled=True)
    pieces = pieces.reshape(adapters, 2, share, width).transpose(1, 2, 0, 3)
    lines = [[near * y + x for x in range(near)] for y in range(lax.axis_size("row") // near)]
    pieces = lax.all_gather(pieces, "row", axis=0, tiled=False, axis_index_groups=lines)
    down = pieces[:, 0].reshape(rank * adapters, width)
    up = pieces[:, 1].reshape(rank * adapters, cols)

    by_core = query_base_weight.reshape(chips // 2, 2, 2, width, cols)
    plain = (jnp.arange(2, dtype=jnp.int32) == core)[None, :, None, None]
    theirs = jnp.where(plain, by_core[:, :, 1], by_core[:, :, 0])
    mine = jnp.where(plain, by_core[:, :, 0], by_core[:, :, 1])
    mine, theirs = lax.optimization_barrier((mine, theirs))
    mine = mine.reshape(chips, width, cols)
    theirs = theirs.reshape(chips, width, cols)
    theirs = with_layout_constraint(theirs, Layout(major_to_minor=(0, 1, 2)))
    partner = lax.ppermute(theirs, "adp", swap)
    partner = with_layout_constraint(partner, Layout(major_to_minor=(0, 1, 2)))

    chosen = (
        row_adapter_index[:, 0][None, :] == jnp.arange(adapters, dtype=jnp.int32)[:, None]
    )
    sums = lax.dot_general(
        down, tokens, (((1,), (1,)), ((), ())), preferred_element_type=jnp.float32
    ).reshape(rank, adapters, rows)
    sums = jnp.where(chosen[None], sums, 0.0).sum(axis=1)
    sums = sums + lax.ppermute(sums, "adp", swap)
    sums = lax.all_gather(sums, "adp", axis=0, tiled=False, axis_index_groups=same_core)
    ranks = sums.sum(axis=0).astype(jnp.bfloat16)
    spread = jnp.where(chosen[None], ranks[:, None, :], jnp.zeros((), jnp.bfloat16))
    update = (
        lax.dot_general(
            spread.reshape(rank * adapters, rows),
            up,
            (((0,), (0,)), ((), ())),
            preferred_element_type=jnp.float32,
        )
        * scale
    ).astype(jnp.bfloat16)
    update = lax.optimization_barrier(update)
    update = with_layout_constraint(update, Layout(major_to_minor=(0, 1)))

    other = _block_sum(gathered, partner)
    other = lax.ppermute(other, "adp", swap)
    own = _block_sum(gathered, mine)
    return (own + other + update.astype(jnp.float32)).astype(jnp.bfloat16)


def solution(mesh):
    return jax.shard_map(
        shards,
        mesh=mesh,
        in_specs=(
            P("row", "adp"),
            P(None, "adp"),
            P("adp", None, None),
            P("adp", None, None),
            P("row", None),
        ),
        out_specs=P("row", "adp"),
        check_vma=False,
    )
```

```python
import jax
import jax.numpy as jnp
from jax import lax
from jax.experimental.layout import Layout, with_layout_constraint
from jax.sharding import PartitionSpec as P

ADAPTER_RANK = 16
SCALE_NUMERATOR = 32


def _block_sum(x, w):
    y = lax.dot_general(
        x, w, (((0, 2), (0, 1)), ((), ())), preferred_element_type=jnp.float32
    )
    return with_layout_constraint(y, Layout(major_to_minor=(0, 1)))


def shards(tokens, query_base_weight, adapter_down_weight, adapter_up_weight, row_adapter_index):
    rows, width = tokens.shape
    _, cols = query_base_weight.shape
    groups = lax.axis_size("adp")
    chips = groups // 2
    rank = adapter_down_weight.shape[1]
    adapters = groups
    core = (lax.axis_index("adp") + lax.axis_index("adp") // 2) % 2
    row = lax.axis_index("row")
    scale = SCALE_NUMERATOR / ADAPTER_RANK
    same_core = [[2 * z + (z + c) % 2 for z in range(chips)] for c in range(2)]
    swap = [(a, a ^ 1) for a in range(groups)]

    gathered = lax.all_gather(tokens, "adp", axis=0, tiled=False, axis_index_groups=same_core)

    near = 4
    share = rank // near
    first = (row % near) * share
    pieces = jnp.stack(
        [
            lax.dynamic_slice_in_dim(adapter_down_weight[0], first, share, 0),
            lax.dynamic_slice_in_dim(adapter_up_weight[0], first, share, 0),
        ]
    )
    pieces = pieces.reshape(2 * share, groups, width).transpose(1, 0, 2)
    pieces = lax.all_to_all(pieces, "adp", split_axis=0, concat_axis=0, tiled=True)
    pieces = pieces.reshape(adapters, 2, share, width).transpose(1, 2, 0, 3)
    lines = [[near * y + x for x in range(near)] for y in range(lax.axis_size("row") // near)]
    pieces = lax.all_gather(pieces, "row", axis=0, tiled=False, axis_index_groups=lines)
    down = pieces[:, 0].reshape(rank * adapters, width)
    up = pieces[:, 1].reshape(rank * adapters, cols)

    by_core = query_base_weight.reshape(chips // 2, 2, 2, width, cols)
    plain = (jnp.arange(2, dtype=jnp.int32) == core)[None, :, None, None]
    theirs = jnp.where(plain, by_core[:, :, 1], by_core[:, :, 0])
    mine = jnp.where(plain, by_core[:, :, 0], by_core[:, :, 1])
    theirs, mine = lax.optimization_barrier((theirs, mine))
    mine = mine.reshape(chips, width, cols)
    theirs = theirs.reshape(chips, width, cols)
    theirs = with_layout_constraint(theirs, Layout(major_to_minor=(0, 1, 2)))
    partner = lax.ppermute(theirs, "adp", swap)
    partner = with_layout_constraint(partner, Layout(major_to_minor=(0, 1, 2)))

    chosen = (
        row_adapter_index[:, 0][None, :] == jnp.arange(adapters, dtype=jnp.int32)[:, None]
    )
    sums = lax.dot_general(
        down, tokens, (((1,), (1,)), ((), ())), preferred_element_type=jnp.float32
    ).reshape(rank, adapters, rows)
    sums = jnp.where(chosen[None], sums, 0.0).sum(axis=1)
    pairs = [[a, a + 1] for a in range(0, groups, 2)]
    sums = lax.all_gather(sums, "adp", axis=0, tiled=False, axis_index_groups=pairs).sum(axis=0)
    part = rows // 2
    sums = lax.dynamic_slice_in_dim(sums, (lax.axis_index("adp") % 2) * part, part, 1)
    sums = lax.all_gather(sums, "adp", axis=0, tiled=False)
    sums = sums.reshape(chips, 2, rank, part).sum(axis=0)
    ranks = sums.transpose(1, 0, 2).reshape(rank, rows).astype(jnp.bfloat16)
    spread = jnp.where(chosen[None], ranks[:, None, :], jnp.zeros((), jnp.bfloat16))
    update = (
        lax.dot_general(
            spread.reshape(rank * adapters, rows),
            up,
            (((0,), (0,)), ((), ())),
            preferred_element_type=jnp.float32,
        )
        * scale
    ).astype(jnp.bfloat16)
    update, gathered = lax.optimization_barrier((update, gathered))
    update = with_layout_constraint(update, Layout(major_to_minor=(0, 1)))

    other = _block_sum(gathered, partner)
    other = lax.ppermute(other, "adp", swap)
    own = _block_sum(gathered, mine)
    return (own + other + update.astype(jnp.float32)).astype(jnp.bfloat16)


def solution(mesh):
    return jax.shard_map(
        shards,
        mesh=mesh,
        in_specs=(
            P("row", "adp"),
            P(None, "adp"),
            P("adp", None, None),
            P("adp", None, None),
            P("row", None),
        ),
        out_specs=P("row", "adp"),
        check_vma=False,
    )
```
